32 devices in a mesh: layer: 4 (over y, x), row: 4 (over z), col: 2 (over core).
Axes of the slice: x: 2, y: 2, z: 4, core: 2. Of those that a mesh axis runs over, the one named last changes fastest.
Arguments:
- density: bfloat16 [2048, 2048], P('row', 'col'), may hold values from -0.5 to 1.5
- pattern: int32 [16, 16], P('row', 'col'), may hold values from 0 to 1, as said below
- holder: int32 [1024, 1], P(('layer', 'row', 'col')), may hold values from 0 to 7; in each aligned block of 32 rows (0 to 31, 32 to 63, ...) at most 8 rows name the same one
- slot_index: int32 [1024], P(('layer', 'row', 'col')), may hold values from 0 to 7
- atom_index: int32 [1024], P(('layer', 'row', 'col')), may hold values from 0 to 7
- derivative: bfloat16 [1024, 3, 128, 128], P(('layer', 'row', 'col')), may hold values from -1.1953125 to 1.1953125
Outputs:
- forces: float32 [3, 256], P(None, ('layer', 'row', 'col'))
The draws below stay inside these ranges and needn't reach their ends.
Inputs may be any that keep to these rules, and one draw needn't show every extreme that they name: `pattern`: the blocks held by one (row, col) grid position form a tile of 4 x 8; in some tile every block is 1. Among the derivative blocks of one device no holder is named more than 8 times, a bound that some block reaches; every holder is named on some device.
All inputs are finite; a program needn't handle non-finite values.
Results may differ from the reference program's by a relative error of at most 0.015.
Values may be sent and summed in bfloat16 or wider, within the bound.
No kernel may reach another device: no remote copies, remote signals or barrier semaphores. Data moves between devices by JAX's collectives and lax.ppermute only.
A program may use at most 128 MiB of HBM per device.

```python
import math
import jax
import jax.numpy as jnp
import numpy as np
from jax import lax

BS = 128
BLK = 4
DER_DEV = 32
ATOM_DEV = 8
NB = 16
N = 2048
TC = 8
HOLD = 8
CAP = 8
ENTRIES = 1024
ATOMS = 256
N_LAYER = 4
N_ROW = 4
N_COL = 2
DEVICES = 32


def draw_density(key, part):
    first_key = jax.random.fold_in(key, 0)
    spread = 0.7 / math.sqrt(N)
    random_part = jax.random.normal(first_key, (N, N), jnp.float32)
    random_part = jnp.clip(random_part, -4.0, 4.0)
    return (0.5 * jnp.eye(N, dtype=jnp.float32) + spread * random_part).astype(jnp.bfloat16)


def draw_pattern(key, part):
    level_key, dense_key, entry_key = jax.random.split(jax.random.fold_in(key, 17), 3)
    levels = jax.random.randint(level_key, (N_ROW, N_COL), 1, 5, dtype=jnp.int32)
    dense_tile = jax.random.randint(dense_key, (), 0, N_ROW * N_COL, dtype=jnp.int32)
    tile_ids = jnp.arange(N_ROW * N_COL, dtype=jnp.int32).reshape(N_ROW, N_COL)
    levels = jnp.where(tile_ids == dense_tile, 4, levels)
    per_block = jnp.repeat(jnp.repeat(levels, BLK, axis=0), TC, axis=1)
    entries = jax.random.randint(entry_key, (NB, NB), 0, 4, dtype=jnp.int32)
    return (entries < per_block).astype(jnp.int32)


def plant(values, own_key, least, largest):
    dims = values.shape
    place = [jax.random.randint(jax.random.fold_in(own_key, axis), (), 0, dims[axis]) for axis in range(len(dims))]
    values = values.at[tuple(place)].set(least)
    longest = dims.index(max(dims))
    place[longest] = (place[longest] + 1) % dims[longest]
    return values.at[tuple(place)].set(largest)


def level_of(key, extent, pieces, least, top_value):
    def one(dim, shards_of):
        draws = jax.random.uniform(jax.random.fold_in(jax.random.fold_in(key, 6), dim), (shards_of,), jnp.float32, least / len(pieces), top_value / len(pieces))
        return jnp.repeat(jnp.exp(draws), extent[dim] // shards_of).reshape((-1,) + (1,) * (len(extent) - dim - 1))

    loudness = one(*pieces[0])
    for cut in pieces[1:]:
        loudness = loudness * one(*cut)
    return loudness


def deal_out(rng, own, number, rows, count, top, reach, lean):
    order = jax.random.permutation(rng, count)
    crowded, ordinary = shares(count, rows * top, reach, lean, True), shares(count, rows * top, reach, lean, False)
    places = jnp.arange(count)

    def named(lengths, turn):
        used = int((lengths > 0).sum())
        fixed = max(1, used // 4)
        shifted = fixed + (places - fixed + turn * (used - fixed)) % max(1, count - fixed)
        return jnp.zeros((count,), jnp.int32).at[order[jnp.where(places < fixed, places, shifted)]].set(jnp.asarray(lengths, jnp.int32))

    lengths = jnp.where(number % 4 == 0, named(crowded, number // 4), named(ordinary, number - number // 4 - 1))
    mixed = jax.random.permutation(jax.random.fold_in(own, 3), count)
    giver, taker = mixed[0:count // 2 * 2:2], mixed[1:count // 2 * 2:2]
    room = jnp.minimum(lengths[giver] - 1, reach - lengths[taker]) // 2
    room = jnp.where((giver == order[0]) | (taker == order[0]) | (lengths[taker] == 0), 0, jnp.maximum(room, 0))
    shifted = jax.random.randint(jax.random.fold_in(own, 4), (count // 2,), 0, 1 << 20) % (room + 1)
    lengths = lengths.at[giver].add(-shifted).at[taker].add(shifted)
    items = jnp.searchsorted(jnp.cumsum(lengths), jnp.arange(rows * top), side="right").astype(jnp.int32)
    grid = items.reshape(top, rows).T
    grid = grid[jax.random.permutation(jax.random.fold_in(own, 1), rows)]
    turn = jax.random.randint(jax.random.fold_in(own, 2), (rows, 1), 0, top)
    return jnp.take_along_axis(grid, (jnp.arange(top)[None, :] + turn) % top, axis=1)


def shares(count, total, limit, skew, full):
    weights = [(1 << 20) // math.isqrt(standing ** skew) + 1 for standing in range(1, count + 1)]
    largest = limit if full else min(limit, max(-(-total // count), total * weights[0] // sum(weights)))
    least = 1 if total - largest >= count - 1 else 0
    holding, rest = [largest] + [least] * (count - 1), total - largest - least * (count - 1)
    while rest > 0:
        free = [i for i in range(1, count) if holding[i] < largest] or [i for i in range(1, count) if holding[i] < limit]
        pool, remaining = sum([weights[i] for i in free]), rest
        for i in free:
            more = min(limit - holding[i], max(1, remaining * weights[i] // pool), rest)
            holding[i] = holding[i] + more
            rest = rest - more
    return np.array(holding)


def scatter_about(key, extent, scale, limit, pieces=(), kind=jnp.bfloat16):
    gain = level_of(key, extent, pieces, -0.22, 0.18) if pieces else 1.0
    drawn = jax.random.normal(key, extent, jnp.float32) * scale * gain
    return jnp.minimum(jnp.maximum(drawn, -limit), limit).astype(kind)


def setup_inputs(seed: int = 0) -> dict:
    splits = jax.random.split(jax.random.key(seed), 7)
    density = draw_density(jax.random.fold_in(splits[6], 71), 0)
    pattern = draw_pattern(jax.random.fold_in(splits[6], 71), 0)
    holder_keys = jax.random.split(jax.random.fold_in(splits[2], 1), ENTRIES // DER_DEV)
    holder_turns = jax.random.permutation(jax.random.fold_in(splits[2], 3), ENTRIES // DER_DEV)
    holder = jax.vmap(lambda own, number: deal_out(jax.random.fold_in(splits[2], 2), own, number, DER_DEV, N_ROW * N_COL, 1, CAP, 2))(holder_keys, holder_turns).reshape((ENTRIES, 1))
    slot_index = plant(jax.random.randint(splits[3], (ENTRIES,), 0, HOLD), jax.random.fold_in(splits[3], 1), 0, HOLD - 1).astype(jnp.int32)
    atom_index = plant(jax.random.randint(splits[4], (ENTRIES,), 0, ATOM_DEV), jax.random.fold_in(splits[4], 1), 0, ATOM_DEV - 1).astype(jnp.int32)
    derivative = scatter_about(splits[5], (ENTRIES, 3, BS, BS), 0.2, 1.1953125, ((0, 32),))
    return {"density": density, "pattern": pattern, "holder": holder, "slot_index": slot_index, "atom_index": atom_index, "derivative": derivative}


def block_filter(matrix, kept_blocks):
    blocked = matrix.reshape(NB, BS, NB, BS)
    return jnp.where(kept_blocks[:, None, :, None], blocked, jnp.zeros_like(blocked)).reshape(N, N)


def reference(density, pattern, holder, slot_index, atom_index, derivative):
    block_ids = jnp.arange(NB, dtype=jnp.int32)
    kept_blocks = (pattern == 1) | (block_ids[:, None] == block_ids[None, :])
    filtered = block_filter(density, kept_blocks)
    square = jnp.dot(filtered, filtered, preferred_element_type=jnp.float32).astype(jnp.bfloat16)
    cube = jnp.dot(square, filtered, preferred_element_type=jnp.float32)
    purified = block_filter(3.0 * square.astype(jnp.float32) - 2.0 * cube, kept_blocks).astype(jnp.bfloat16)
    blocked = purified.reshape(NB, BS, NB, BS)
    col_blocks = NB // N_COL
    owners = jnp.arange(ENTRIES, dtype=jnp.int32) // DER_DEV
    layer_ids = owners // (N_ROW * N_COL)
    holders = holder[:, 0]
    block_row = (holders // N_COL) * BLK + layer_ids * (BLK // N_LAYER) + slot_index // col_blocks
    block_col = (holders % N_COL) * col_blocks + slot_index % col_blocks

    def per_owner(inputs):
        rows_here, cols_here, atoms_here, deriv_here = inputs
        picked = blocked[rows_here, :, cols_here, :]
        contrib = jnp.einsum("eij,exij->xe", picked.astype(jnp.float32), deriv_here.astype(jnp.float32), precision=lax.Precision.HIGHEST)
        atom_hot = (atoms_here[:, None] == jnp.arange(ATOM_DEV, dtype=jnp.int32)[None, :]).astype(jnp.float32)
        return -2.0 * jnp.dot(contrib, atom_hot, precision=lax.Precision.HIGHEST)

    stacked = lax.map(per_owner, (block_row.reshape(DEVICES, DER_DEV), block_col.reshape(DEVICES, DER_DEV), atom_index.reshape(DEVICES, DER_DEV), derivative.reshape(DEVICES, DER_DEV, 3, BS, BS)))
    return jnp.transpose(stacked, (1, 0, 2)).reshape(3, ATOMS)
```

```python
import functools

import jax
import jax.numpy as jnp
from jax import lax
from jax.experimental import pallas as pl
from jax.experimental.pallas import tpu as pltpu
from jax.sharding import PartitionSpec as P


BS = 128
ATOM_DEV = 8
RESIDENT_GRID = (4, 4, 2)
ALONG_X, ALONG_Y = 1, 2


def block_filter(matrix, kept_blocks):
    count_rows, count_cols = kept_blocks.shape
    blocked = matrix.reshape(count_rows, BS, count_cols, BS)
    return jnp.where(kept_blocks[:, None, :, None], blocked, jnp.zeros_like(blocked)).reshape(
        matrix.shape
    )


def column_subset(matrix, layer_count, layer_id):
    reshaped = matrix.reshape(matrix.shape[0], -1, layer_count, BS)
    picked = lax.dynamic_index_in_dim(reshaped, layer_id, 2, keepdims=False)
    return picked.reshape(matrix.shape[0], -1)


def row_subset(matrix, layer_count, layer_id):
    reshaped = matrix.reshape(-1, layer_count, BS, matrix.shape[1])
    picked = lax.dynamic_index_in_dim(reshaped, layer_id, 1, keepdims=False)
    return picked.reshape(-1, matrix.shape[1])


def multiply(left_matrix, right_matrix, layer_count, layer_id):
    left_part = column_subset(left_matrix, layer_count, layer_id)
    right_part = row_subset(right_matrix, layer_count, layer_id)
    row_strip = lax.all_gather(right_part, "row", axis=0, tiled=True)
    return jnp.dot(
        lax.all_gather(left_part, "col", axis=1, tiled=True),
        row_strip,
        preferred_element_type=jnp.float32,
    )


def split_shards(density, pattern, holder, slot_index, atom_index, derivative):
    layer_count = lax.axis_size("layer")
    layer_id = lax.axis_index("layer")
    grid_row = lax.axis_index("row")
    grid_col = lax.axis_index("col")
    row_blocks, col_blocks = pattern.shape
    global_rows = grid_row * row_blocks + jnp.arange(row_blocks, dtype=jnp.int32)
    global_cols = grid_col * col_blocks + jnp.arange(col_blocks, dtype=jnp.int32)
    kept_blocks = (pattern == 1) | (global_rows[:, None] == global_cols[None, :])
    filtered = block_filter(density, kept_blocks)
    partial_square = multiply(filtered, filtered, layer_count, layer_id)
    share_blocks = row_blocks // layer_count
    square_share = lax.psum_scatter(
        partial_square, "layer", scatter_dimension=0, tiled=True
    ).astype(jnp.bfloat16)
    square = lax.all_gather(square_share, "layer", axis=0, tiled=True)
    partial_cube = multiply(square, filtered, layer_count, layer_id)
    cube_share = lax.psum_scatter(partial_cube, "layer", scatter_dimension=0, tiled=True)
    kept_share = lax.dynamic_slice_in_dim(kept_blocks, layer_id * share_blocks, share_blocks, 0)
    purified = block_filter(
        3.0 * square_share.astype(jnp.float32) - 2.0 * cube_share, kept_share
    ).astype(jnp.bfloat16)
    held_blocks = (
        purified.reshape(share_blocks, BS, col_blocks, BS)
        .transpose(0, 2, 1, 3)
        .reshape(share_blocks * col_blocks, BS, BS)
    )
    holders_total = lax.axis_size("row") * lax.axis_size("col")
    entry_count = slot_index.shape[0]
    capacity = max(2, 2 * entry_count // holders_total)
    targets = holder[:, 0]
    target_hot = (targets[:, None] == jnp.arange(holders_total, dtype=jnp.int32)[None, :]).astype(
        jnp.int32
    )
    rank_values = jnp.sum(target_hot * (jnp.cumsum(target_hot, axis=0) - 1), axis=1)
    positions = targets * capacity + rank_values
    position_hot = (
        positions[None, :] == jnp.arange(holders_total * capacity, dtype=jnp.int32)[:, None]
    )
    requests = jnp.sum(jnp.where(position_hot, slot_index[None, :], 0), axis=1).reshape(
        holders_total, capacity
    )
    fetched = jnp.take(
        held_blocks,
        lax.all_to_all(requests, ("row", "col"), split_axis=0, concat_axis=0, tiled=True),
        axis=0,
    )
    returned = lax.all_to_all(fetched, ("row", "col"), split_axis=0, concat_axis=0, tiled=True)
    arrived = jnp.take(returned.reshape(holders_total * capacity, BS, BS), positions, axis=0)
    contrib = jnp.einsum("eij,exij->xe", arrived, derivative, preferred_element_type=jnp.float32)
    atom_hot = (atom_index[:, None] == jnp.arange(ATOM_DEV, dtype=jnp.int32)[None, :]).astype(
        jnp.float32
    )
    return -2.0 * jnp.dot(contrib, atom_hot, precision=lax.Precision.HIGHEST)


def positions_of():
    return lax.axis_index("layer"), lax.axis_index("row"), lax.axis_index("col")


def kept_block(pattern_ref, row, column, grid_row, grid_col):
    row_blocks, col_blocks = pattern_ref.shape
    diagonal = grid_row * row_blocks + row == grid_col * col_blocks + column
    return (pattern_ref[row, column] == 1) | diagonal


def clear_blocks(out, pattern_ref, first, count, grid_row, grid_col):
    for i in range(count):
        for q in range(pattern_ref.shape[1]):
            kept = kept_block(pattern_ref, first + i, q, grid_row, grid_col)

            @pl.when(jnp.logical_not(kept))
            def _():
                out[i * BS : (i + 1) * BS, q * BS : (q + 1) * BS] = jnp.zeros((BS, BS), out.dtype)


def unit_kernel(share, density_ref, source_ref, out_ref, pattern_ref, sems):
    layer_id, grid_row, grid_col = positions_of()
    rows = share * BS
    copies = []
    begin(copies, source_ref, pattern_ref, sems.at[0])
    start = pl.multiple_of(layer_id * rows, rows)
    begin(copies, density_ref.at[pl.ds(start, rows), :], out_ref, sems.at[1])
    for copy in copies:
        copy.wait()
    clear_blocks(out_ref, pattern_ref, layer_id * share, share, grid_row, grid_col)


def filter_kernel(share, far, density_ref, *refs):
    source_refs, refs = refs[:-6], refs[-6:]
    out_ref, far_ref, full, patterns_ref, pattern_ref, sems = refs
    layer_id, grid_row, grid_col = positions_of()
    rows = share * BS
    unit = layer_id ^ far
    row_blocks, col_blocks = pattern_ref.shape
    own = full.at[
        pl.ds(pl.multiple_of(grid_row * row_blocks * BS, row_blocks * BS), row_blocks * BS),
        pl.ds(pl.multiple_of(grid_col * col_blocks * BS, col_blocks * BS), col_blocks * BS),
    ]
    copies = []
    begin(copies, source_refs[0], pattern_ref, sems.at[0])
    for k, ref in enumerate(source_refs):
        begin(copies, ref, patterns_ref.at[k], sems.at[4 + k])
    begin(copies, density_ref, out_ref, sems.at[1])
    begin(copies, density_ref, own, sems.at[2])
    start = pl.multiple_of(unit * rows, rows)
    begin(copies, density_ref.at[pl.ds(start, rows), :], far_ref, sems.at[3])
    for copy in copies:
        copy.wait()
    clear_blocks(far_ref, pattern_ref, unit * share, share, grid_row, grid_col)
    for out in (out_ref, own):
        clear_blocks(out, pattern_ref, 0, row_blocks, grid_row, grid_col)


def begin(copies, source, target, sem):
    copies.append(pltpu.make_async_copy(source, target, sem))
    copies[-1].start()


def flip_of(kind, core):
    if kind == "a":
        return ALONG_X + core * (ALONG_Y - ALONG_X)
    if kind == "b":
        return ALONG_Y + core * (ALONG_X - ALONG_Y)
    return kind


def unit_start(layer_id, grid_row, core, unit, row_blocks, rows):
    d, kind = unit
    first = (grid_row ^ d) * row_blocks * BS
    return first if kind is None else first + (layer_id ^ flip_of(kind, core)) * rows


def square_kernel(layout, pairs, absent, share, row_blocks, col_blocks, *refs):
    count = len(layout)
    unit_refs, refs = refs[:count], refs[count:]
    first = len(refs) == 6
    if first:
        _, full, left, partial, sems, left_sems = refs
    else:
        _, _, left, full, partial, sems, left_sems = refs
    layer_id, grid_row, grid_col = positions_of()
    rows = share * BS
    width = col_blocks * BS
    copies = []
    for slot, (ref, (unit, half, placed)) in enumerate(zip(unit_refs, layout)):
        core = grid_col ^ half
        columns = pl.ds(pl.multiple_of(core * width, width), width)
        if not placed:
            height = ref.shape[0]
            start = unit_start(layer_id, grid_row, core, unit, row_blocks, rows)
            start = pl.multiple_of(start, height)
            begin(copies, ref, full.at[pl.ds(start, height), columns], sems.at[slot])
        if first and not unit[1]:
            source = ref
            if unit[1] is None:
                source = ref.at[pl.ds(pl.multiple_of(layer_id * rows, rows), rows), :]
            start = pl.multiple_of((grid_row ^ unit[0]) * rows, rows)
            begin(copies, source, left.at[pl.ds(start, rows), columns], left_sems.at[slot])
    for unit in absent:
        start = unit_start(layer_id, grid_row, grid_col, unit, row_blocks, rows)
        full[pl.ds(pl.multiple_of(start, rows), rows), :] = jnp.zeros(
            (rows, full.shape[1]), full.dtype
        )
    for copy in copies:
        copy.wait()
    depth = 2 * rows
    total = None if first else partial[...]
    for d, flip in pairs:
        start = (grid_row ^ d) * row_blocks * BS + (layer_id ^ flip) // 2 * depth
        k = pl.ds(pl.multiple_of(start, depth), depth)
        more = jnp.dot(left[:, k], full[k, :], preferred_element_type=jnp.float32)
        total = more if total is None else total + more
    partial[...] = total


def force_kernel(late, absent, n_rows, n_cols, share, row_blocks, col_blocks, *refs):
    tables, refs = refs[:5], refs[5:]
    late_refs, refs = refs[: len(late)], refs[len(late) :]
    (
        full_ref,
        left,
        partial,
        held,
        forces_ref,
        full,
        square,
        purified,
        last,
        last_left,
        totals,
        kept,
        holder_ref,
        slot_ref,
        atom_ref,
        patterns_ref,
        sems,
        table_sems,
    ) = refs
    del full_ref
    layer_id, grid_row, grid_col = positions_of()
    rows = share * BS
    width = col_blocks * BS
    copies = []
    for k, (ref, (unit, half)) in enumerate(zip(late_refs, late)):
        core = grid_col ^ half
        column = pl.multiple_of(core * width, width)
        place = absent.index(unit) * rows
        begin(copies, ref, last.at[pl.ds(place, rows), pl.ds(column, width)], sems.at[k])
    places = [holder_ref, slot_ref, atom_ref, patterns_ref.at[0], patterns_ref.at[1]]
    table_copies = []
    for k, (table, place) in enumerate(zip(tables, places)):
        begin(table_copies, table, place, table_sems.at[k])
    totals[...] = jnp.zeros_like(totals)
    starts = [
        pl.multiple_of(unit_start(layer_id, grid_row, grid_col, unit, row_blocks, rows), rows)
        for unit in absent
    ]
    for k, start in enumerate(starts):
        last_left[:, k * rows : (k + 1) * rows] = left[:, pl.ds(start, rows)]
    for copy in copies:
        copy.wait()
    for k, start in enumerate(starts):
        full[pl.ds(start, rows), :] = last[k * rows : (k + 1) * rows, :]
    more = jnp.dot(last_left[...], last[...], preferred_element_type=jnp.float32)
    square[...] = (partial[...] + more).astype(square.dtype)
    cube = jnp.dot(square[...], full[...], preferred_element_type=jnp.float32)
    purified[...] = (3.0 * square[...].astype(jnp.float32) - 2.0 * cube).astype(purified.dtype)

    for copy in table_copies:
        copy.wait()
    for half in range(2):
        for d in range(n_rows):
            pattern_ref = patterns_ref.at[half, d]
            place, column = grid_row ^ d, grid_col ^ half
            for i in range(share):
                for q in range(col_blocks):
                    value = kept_block(pattern_ref, layer_id * share + i, q, place, column)
                    kept[place * share + i, column * col_blocks + q] = value.astype(jnp.int32)

    @pl.loop(0, held.shape[0], unroll=4)
    def _(e):
        h = holder_ref[e]
        s = slot_ref[e]
        row = (h // n_cols) * share + s // col_blocks
        column = (h % n_cols) * col_blocks + s % col_blocks
        block = purified[
            pl.ds(pl.multiple_of(row * BS, BS), BS), pl.ds(pl.multiple_of(column * BS, BS), BS)
        ].astype(jnp.float32)

        keep = kept[row, column] == 1
        for x in range(held.shape[1]):
            product = block * held[e, x].astype(jnp.float32)
            part = jnp.sum(product.reshape(BS // 8, 8, BS), axis=0)
            part = jnp.where(keep, part, jnp.zeros_like(part))
            totals[x, atom_ref[e]] = totals[x, atom_ref[e]] + part

    sums = jnp.sum(jnp.sum(totals[...], axis=3), axis=2)
    forces_ref[...] = -2.0 * sums


VMEM = pl.BlockSpec(memory_space=pltpu.VMEM)
SMEM = pl.BlockSpec(memory_space=pltpu.SMEM)
ANY = pl.BlockSpec(memory_space=pl.ANY)
HBM = pl.BlockSpec(memory_space=pltpu.HBM)


def resident_step(sizes, density, pattern, holder, slot_index, atom_index, derivative):
    layers, n_rows, n_cols = sizes
    row_blocks, col_blocks = pattern.shape
    share = row_blocks // layers
    rows = share * BS
    width = n_cols * col_blocks * BS
    height = n_rows * row_blocks * BS
    tall = n_rows * rows
    dtype = density.dtype
    grid_row = lax.axis_index("row")
    outer = n_rows - 1
    inner = (grid_row != 0) & (grid_row != outer)
    middle = tuple(range(1, outer))

    def send(value, axis, flip, only=None):
        pairs = [
            (i, i ^ flip) for i in range(lax.axis_size(axis)) if only is None or i in only
        ]
        return lax.ppermute(value, axis, pairs)

    def spread(value, kind):
        pairs = [
            (g * n_cols + c, (g ^ flip_of(kind, c)) * n_cols + c)
            for g in range(layers)
            for c in range(n_cols)
        ]
        return lax.ppermute(value, ("layer", "col"), pairs)

    masks = pltpu.SMEM(pattern.shape, pattern.dtype)
    full_shape = jax.ShapeDtypeStruct((height, width), dtype)
    unit_shape = jax.ShapeDtypeStruct((rows, density.shape[1]), dtype)
    near = pl.pallas_call(
        functools.partial(unit_kernel, share),
        out_shape=unit_shape,
        in_specs=[ANY, ANY],
        out_specs=VMEM,
        scratch_shapes=[masks, pltpu.SemaphoreType.DMA((2,))],
        name="unit",
    )(density, pattern)
    filter_call = pl.pallas_call(
        functools.partial(filter_kernel, share, ALONG_X ^ ALONG_Y),
        out_shape=[
            jax.ShapeDtypeStruct(density.shape, dtype),
            unit_shape,
            full_shape,
            jax.ShapeDtypeStruct((n_rows,) + pattern.shape, pattern.dtype),
        ],
        in_specs=[ANY] * (1 + n_rows),
        out_specs=[VMEM] * 4,
        scratch_shapes=[masks, pltpu.SemaphoreType.DMA((4 + n_rows,))],
        compiler_params=pltpu.CompilerParams(vmem_limit_bytes=16 * 2**20),
        name="filter",
    )
    patterns = [pattern] + [send(pattern, "row", d) for d in range(1, n_rows)]
    filtered, far, full, patterns = filter_call(density, *patterns)
    other_patterns = send(patterns, "col", 1)
    other = send(filtered, "col", 1)

    z1 = send(near, "row", 1)
    b = send(near, "row", outer, middle)
    d = send(z1, "row", outer, middle)
    c = send(b, "row", 1, middle)
    e = send(d, "row", 1, middle)
    z2 = jnp.where(inner, d, c)
    z3 = jnp.where(inner, b, e)

    diagonal = ALONG_X ^ ALONG_Y
    absent = ((3, diagonal),)
    placed = [((0, 0), 0, True, near), ((0, None), 1, False, other)]
    late = []
    for k, z in ((1, z1), (2, z2), (3, z3)):
        a_ = spread(z, "a")
        b_ = spread(z, "b")
        w_ = send(far, "row", 1) if k == 1 else spread(a_, "b")
        for kind, value in ((0, z), ("a", a_), ("b", b_), (diagonal, w_)):
            partner = send(value, "col", 1)
            for half, part in enumerate((value, partner)):
                if (k, kind) in absent:
                    late.append(((k, kind), half, part))
                else:
                    placed.append(((k, kind), half, False, part))
    left_shape = jax.ShapeDtypeStruct((tall, width), dtype)
    partial_shape = jax.ShapeDtypeStruct((tall, width), jnp.float32)

    def add_squares(units, pairs, zeros, full, *held):
        count = len(units)
        layout = tuple(u[:3] for u in units)
        return pl.pallas_call(
            functools.partial(square_kernel, layout, pairs, zeros, share, row_blocks, col_blocks),
            out_shape=[full_shape] + ([] if held else [left_shape]) + [partial_shape],
            in_specs=[HBM] * count + [VMEM] * (1 + len(held)),
            out_specs=[VMEM] * (2 if held else 3),
            input_output_aliases={count: 0, count + 1: 1} if held else {count: 0},
            scratch_shapes=[pltpu.SemaphoreType.DMA((count,))] * 2,
            compiler_params=pltpu.CompilerParams(vmem_limit_bytes=24 * 2**20),
        )(*[u[3] for u in units], full, *held)

    behind = ((1, diagonal), (2, diagonal), (3, "a"), (3, "b"))
    early = [u for u in placed if u[0] not in behind]
    later = [u for u in placed if u[0] in behind]
    full, left, partial = add_squares(early, ((0, 0), (0, ALONG_Y), (1, 0), (2, 0)), (), full)
    full, partial = add_squares(
        later, ((1, ALONG_Y), (2, ALONG_Y), (3, 0), (3, ALONG_Y)), absent, full, partial, left
    )
    tables = [holder.reshape(-1), slot_index, atom_index, patterns, other_patterns]
    n_late = len(late)
    components = derivative.shape[1]
    return pl.pallas_call(
        functools.partial(
            force_kernel,
            tuple(u[:2] for u in late),
            absent,
            n_rows,
            n_cols,
            share,
            row_blocks,
            col_blocks,
        ),
        out_shape=[jax.ShapeDtypeStruct((components, ATOM_DEV), jnp.float32), full_shape],
        in_specs=[ANY] * len(tables) + [HBM] * n_late + [VMEM] * 4,
        out_specs=[VMEM] * 2,
        input_output_aliases={len(tables) + n_late: 1},
        scratch_shapes=[
            pltpu.VMEM((tall, width), dtype),
            pltpu.VMEM((tall, width), dtype),
            pltpu.VMEM((len(absent) * rows, width), dtype),
            pltpu.VMEM((tall, len(absent) * rows), dtype),
            pltpu.VMEM((components, ATOM_DEV, 8, BS), jnp.float32),
            pltpu.SMEM((n_rows * share, n_cols * col_blocks), jnp.int32),
            pltpu.SMEM(slot_index.shape, jnp.int32),
            pltpu.SMEM(slot_index.shape, jnp.int32),
            pltpu.SMEM(slot_index.shape, jnp.int32),
            pltpu.SMEM((2, n_rows) + pattern.shape, jnp.int32),
            pltpu.SemaphoreType.DMA((n_late,)),
            pltpu.SemaphoreType.DMA((len(tables),)),
        ],
        compiler_params=pltpu.CompilerParams(vmem_limit_bytes=24 * 2**20),
        name="force",
    )(*tables, *[u[2] for u in late], full, left, partial, derivative)[0]


def resident_fits(mesh):
    return tuple(mesh.shape[axis] for axis in ("layer", "row", "col")) == RESIDENT_GRID


def solution(mesh):
    specs = dict(
        mesh=mesh,
        in_specs=(
            P("row", "col"),
            P("row", "col"),
            P(("layer", "row", "col"), None),
            P(("layer", "row", "col")),
            P(("layer", "row", "col")),
            P(("layer", "row", "col"), None, None, None),
        ),
        out_specs=P(None, ("layer", "row", "col")),
        check_vma=False,
    )
    if not resident_fits(mesh):
        return jax.shard_map(split_shards, **specs)
    sizes = tuple(mesh.shape[axis] for axis in ("layer", "row", "col"))

    def shards(*args):
        return resident_step(sizes, *args)

    return jax.shard_map(shards, **specs)
```

```python
import functools

import jax
import jax.numpy as jnp
from jax import lax
from jax.experimental import pallas as pl
from jax.experimental.pallas import tpu as pltpu
from jax.sharding import PartitionSpec as P


BS = 128
ATOM_DEV = 8
RESIDENT_GRID = (4, 4, 2)
ALONG_X, ALONG_Y = 1, 2
UNROLL = 8


def block_filter(matrix, kept_blocks):
    count_rows, count_cols = kept_blocks.shape
    blocked = matrix.reshape(count_rows, BS, count_cols, BS)
    return jnp.where(kept_blocks[:, None, :, None], blocked, jnp.zeros_like(blocked)).reshape(
        matrix.shape
    )


def column_subset(matrix, layer_count, layer_id):
    reshaped = matrix.reshape(matrix.shape[0], -1, layer_count, BS)
    picked = lax.dynamic_index_in_dim(reshaped, layer_id, 2, keepdims=False)
    return picked.reshape(matrix.shape[0], -1)


def row_subset(matrix, layer_count, layer_id):
    reshaped = matrix.reshape(-1, layer_count, BS, matrix.shape[1])
    picked = lax.dynamic_index_in_dim(reshaped, layer_id, 1, keepdims=False)
    return picked.reshape(-1, matrix.shape[1])


def multiply(left_matrix, right_matrix, layer_count, layer_id):
    left_part = column_subset(left_matrix, layer_count, layer_id)
    right_part = row_subset(right_matrix, layer_count, layer_id)
    row_strip = lax.all_gather(right_part, "row", axis=0, tiled=True)
    return jnp.dot(
        lax.all_gather(left_part, "col", axis=1, tiled=True),
        row_strip,
        preferred_element_type=jnp.float32,
    )


def split_shards(density, pattern, holder, slot_index, atom_index, derivative):
    layer_count = lax.axis_size("layer")
    layer_id = lax.axis_index("layer")
    grid_row = lax.axis_index("row")
    grid_col = lax.axis_index("col")
    row_blocks, col_blocks = pattern.shape
    global_rows = grid_row * row_blocks + jnp.arange(row_blocks, dtype=jnp.int32)
    global_cols = grid_col * col_blocks + jnp.arange(col_blocks, dtype=jnp.int32)
    kept_blocks = (pattern == 1) | (global_rows[:, None] == global_cols[None, :])
    filtered = block_filter(density, kept_blocks)
    partial_square = multiply(filtered, filtered, layer_count, layer_id)
    share_blocks = row_blocks // layer_count
    square_share = lax.psum_scatter(
        partial_square, "layer", scatter_dimension=0, tiled=True
    ).astype(jnp.bfloat16)
    square = lax.all_gather(square_share, "layer", axis=0, tiled=True)
    partial_cube = multiply(square, filtered, layer_count, layer_id)
    cube_share = lax.psum_scatter(partial_cube, "layer", scatter_dimension=0, tiled=True)
    kept_share = lax.dynamic_slice_in_dim(kept_blocks, layer_id * share_blocks, share_blocks, 0)
    purified = block_filter(
        3.0 * square_share.astype(jnp.float32) - 2.0 * cube_share, kept_share
    ).astype(jnp.bfloat16)
    held_blocks = (
        purified.reshape(share_blocks, BS, col_blocks, BS)
        .transpose(0, 2, 1, 3)
        .reshape(share_blocks * col_blocks, BS, BS)
    )
    holders_total = lax.axis_size("row") * lax.axis_size("col")
    entry_count = slot_index.shape[0]
    capacity = max(2, 2 * entry_count // holders_total)
    targets = holder[:, 0]
    target_hot = (targets[:, None] == jnp.arange(holders_total, dtype=jnp.int32)[None, :]).astype(
        jnp.int32
    )
    rank_values = jnp.sum(target_hot * (jnp.cumsum(target_hot, axis=0) - 1), axis=1)
    positions = targets * capacity + rank_values
    position_hot = (
        positions[None, :] == jnp.arange(holders_total * capacity, dtype=jnp.int32)[:, None]
    )
    requests = jnp.sum(jnp.where(position_hot, slot_index[None, :], 0), axis=1).reshape(
        holders_total, capacity
    )
    fetched = jnp.take(
        held_blocks,
        lax.all_to_all(requests, ("row", "col"), split_axis=0, concat_axis=0, tiled=True),
        axis=0,
    )
    returned = lax.all_to_all(fetched, ("row", "col"), split_axis=0, concat_axis=0, tiled=True)
    arrived = jnp.take(returned.reshape(holders_total * capacity, BS, BS), positions, axis=0)
    contrib = jnp.einsum("eij,exij->xe", arrived, derivative, preferred_element_type=jnp.float32)
    atom_hot = (atom_index[:, None] == jnp.arange(ATOM_DEV, dtype=jnp.int32)[None, :]).astype(
        jnp.float32
    )
    return -2.0 * jnp.dot(contrib, atom_hot, precision=lax.Precision.HIGHEST)


def positions_of():
    return lax.axis_index("layer"), lax.axis_index("row"), lax.axis_index("col")


def kept_block(pattern_ref, row, column, grid_row, grid_col):
    row_blocks, col_blocks = pattern_ref.shape
    diagonal = grid_row * row_blocks + row == grid_col * col_blocks + column
    return (pattern_ref[row, column] == 1) | diagonal


def clear_blocks(out, pattern_ref, first, count, grid_row, grid_col):
    for i in range(count):
        for q in range(pattern_ref.shape[1]):
            kept = kept_block(pattern_ref, first + i, q, grid_row, grid_col)

            @pl.when(jnp.logical_not(kept))
            def _():
                out[i * BS : (i + 1) * BS, q * BS : (q + 1) * BS] = jnp.zeros((BS, BS), out.dtype)


def unit_kernel(share, density_ref, source_ref, out_ref, pattern_ref, sems):
    layer_id, grid_row, grid_col = positions_of()
    rows = share * BS
    copies = []
    begin(copies, source_ref, pattern_ref, sems.at[0])
    start = pl.multiple_of(layer_id * rows, rows)
    begin(copies, density_ref.at[pl.ds(start, rows), :], out_ref, sems.at[1])
    for copy in copies:
        copy.wait()
    clear_blocks(out_ref, pattern_ref, layer_id * share, share, grid_row, grid_col)


def filter_kernel(share, far, density_ref, *refs):
    source_refs, refs = refs[:-6], refs[-6:]
    out_ref, far_ref, full, patterns_ref, pattern_ref, sems = refs
    layer_id, grid_row, grid_col = positions_of()
    rows = share * BS
    unit = layer_id ^ far
    row_blocks, col_blocks = pattern_ref.shape
    own = full.at[
        pl.ds(pl.multiple_of(grid_row * row_blocks * BS, row_blocks * BS), row_blocks * BS),
        pl.ds(pl.multiple_of(grid_col * col_blocks * BS, col_blocks * BS), col_blocks * BS),
    ]
    copies = []
    begin(copies, source_refs[0], pattern_ref, sems.at[0])
    for k, ref in enumerate(source_refs):
        begin(copies, ref, patterns_ref.at[k], sems.at[4 + k])
    begin(copies, density_ref, out_ref, sems.at[1])
    begin(copies, density_ref, own, sems.at[2])
    start = pl.multiple_of(unit * rows, rows)
    begin(copies, density_ref.at[pl.ds(start, rows), :], far_ref, sems.at[3])
    for copy in copies:
        copy.wait()
    clear_blocks(far_ref, pattern_ref, unit * share, share, grid_row, grid_col)
    for out in (out_ref, own):
        clear_blocks(out, pattern_ref, 0, row_blocks, grid_row, grid_col)


def begin(copies, source, target, sem):
    copies.append(pltpu.make_async_copy(source, target, sem))
    copies[-1].start()


def flip_of(kind, core):
    if kind == "a":
        return ALONG_X + core * (ALONG_Y - ALONG_X)
    if kind == "b":
        return ALONG_Y + core * (ALONG_X - ALONG_Y)
    return kind


def unit_start(layer_id, grid_row, core, unit, row_blocks, rows):
    d, kind = unit
    first = (grid_row ^ d) * row_blocks * BS
    return first if kind is None else first + (layer_id ^ flip_of(kind, core)) * rows


def square_kernel(layout, pairs, absent, share, row_blocks, col_blocks, *refs):
    count = len(layout)
    unit_refs, refs = refs[:count], refs[count:]
    first = len(refs) == 6
    if first:
        _, full, left, partial, sems, left_sems = refs
    else:
        _, _, left, full, partial, sems, left_sems = refs
    layer_id, grid_row, grid_col = positions_of()
    rows = share * BS
    width = col_blocks * BS
    copies = []
    for slot, (ref, (unit, half)) in enumerate(zip(unit_refs, layout)):
        core = grid_col ^ half
        columns = pl.ds(pl.multiple_of(core * width, width), width)
        height = ref.shape[0]
        start = unit_start(layer_id, grid_row, core, unit, row_blocks, rows)
        start = pl.multiple_of(start, height)
        begin(copies, ref, full.at[pl.ds(start, height), columns], sems.at[slot])
        if first and not unit[1]:
            source = ref
            if unit[1] is None:
                source = ref.at[pl.ds(pl.multiple_of(layer_id * rows, rows), rows), :]
            start = pl.multiple_of((grid_row ^ unit[0]) * rows, rows)
            begin(copies, source, left.at[pl.ds(start, rows), columns], left_sems.at[slot])
    if first:
        start = unit_start(layer_id, grid_row, grid_col, (0, 0), row_blocks, rows)
        columns = pl.ds(pl.multiple_of(grid_col * width, width), width)
        source = full.at[pl.ds(pl.multiple_of(start, rows), rows), columns]
        start = pl.multiple_of(grid_row * rows, rows)
        begin(copies, source, left.at[pl.ds(start, rows), columns], left_sems.at[count])
    for unit in absent:
        start = unit_start(layer_id, grid_row, grid_col, unit, row_blocks, rows)
        full[pl.ds(pl.multiple_of(start, rows), rows), :] = jnp.zeros(
            (rows, full.shape[1]), full.dtype
        )
    for copy in copies:
        copy.wait()
    depth = 2 * rows
    total = None if first else partial[...]
    for d, flip in pairs:
        start = (grid_row ^ d) * row_blocks * BS + (layer_id ^ flip) // 2 * depth
        k = pl.ds(pl.multiple_of(start, depth), depth)
        more = jnp.dot(left[:, k], full[k, :], preferred_element_type=jnp.float32)
        total = more if total is None else total + more
    partial[...] = total


def force_kernel(late, absent, n_cols, share, row_blocks, col_blocks, *refs):
    tables, refs = refs[:5], refs[5:]
    late_refs, refs = refs[: len(late)], refs[len(late) :]
    (
        full_ref,
        left,
        partial,
        held,
        forces_ref,
        full,
        square,
        purified,
        last,
        last_left,
        totals,
        holder_ref,
        slot_ref,
        atom_ref,
        patterns_ref,
        sems,
        table_sems,
    ) = refs
    del full_ref
    layer_id, grid_row, grid_col = positions_of()
    rows = share * BS
    width = col_blocks * BS
    copies = []
    for k, (ref, (unit, half)) in enumerate(zip(late_refs, late)):
        core = grid_col ^ half
        column = pl.multiple_of(core * width, width)
        place = absent.index(unit) * rows
        begin(copies, ref, last.at[pl.ds(place, rows), pl.ds(column, width)], sems.at[k])
    places = [holder_ref, slot_ref, atom_ref, patterns_ref.at[0], patterns_ref.at[1]]
    table_copies = []
    for k, (table, place) in enumerate(zip(tables, places)):
        begin(table_copies, table, place, table_sems.at[k])
    starts = [
        pl.multiple_of(unit_start(layer_id, grid_row, grid_col, unit, row_blocks, rows), rows)
        for unit in absent
    ]
    for k, start in enumerate(starts):
        last_left[:, k * rows : (k + 1) * rows] = left[:, pl.ds(start, rows)]
    for copy in copies:
        copy.wait()
    for k, start in enumerate(starts):
        full[pl.ds(start, rows), :] = last[k * rows : (k + 1) * rows, :]
    more = jnp.dot(last_left[...], last[...], preferred_element_type=jnp.float32)
    square[...] = (partial[...] + more).astype(square.dtype)
    cube = jnp.dot(square[...], full[...], preferred_element_type=jnp.float32)
    purified[...] = (3.0 * square[...].astype(jnp.float32) - 2.0 * cube).astype(purified.dtype)
    for copy in table_copies:
        copy.wait()
    components = held.shape[1]

    totals[...] = jnp.zeros_like(totals)

    @pl.loop(0, held.shape[0], unroll=UNROLL)
    def _(e):
        h = holder_ref[e]
        s = slot_ref[e]
        place, core = h // n_cols, h % n_cols
        row, column = s // col_blocks, s % col_blocks
        tile_row = layer_id * share + row
        pattern = patterns_ref[core ^ grid_col, place ^ grid_row, tile_row, column]
        across = core * col_blocks + column
        keep = (pattern == 1) | (place * row_blocks + tile_row == across)
        rows_at = pl.ds(pl.multiple_of((place * share + row) * BS, BS), BS)
        columns_at = pl.ds(pl.multiple_of(across * BS, BS), BS)
        block = purified[rows_at, columns_at].astype(jnp.float32)
        atom = atom_ref[e]
        for x in range(components):
            product = block * held[e, x].astype(jnp.float32)
            part = jnp.sum(product.reshape(BS // 8, 8, BS), axis=0)
            part = jnp.where(keep, part, jnp.zeros_like(part))
            totals[x, atom] = totals[x, atom] + part

    forces_ref[...] = -2.0 * jnp.sum(jnp.sum(totals[...], axis=3), axis=2)


VMEM = pl.BlockSpec(memory_space=pltpu.VMEM)
SMEM = pl.BlockSpec(memory_space=pltpu.SMEM)
ANY = pl.BlockSpec(memory_space=pl.ANY)
HBM = pl.BlockSpec(memory_space=pltpu.HBM)


def resident_step(sizes, density, pattern, holder, slot_index, atom_index, derivative):
    layers, n_rows, n_cols = sizes
    row_blocks, col_blocks = pattern.shape
    share = row_blocks // layers
    rows = share * BS
    width = n_cols * col_blocks * BS
    height = n_rows * row_blocks * BS
    tall = n_rows * rows
    dtype = density.dtype
    grid_row = lax.axis_index("row")
    outer = n_rows - 1
    inner = (grid_row != 0) & (grid_row != outer)
    middle = tuple(range(1, outer))

    def send(value, axis, flip, only=None):
        pairs = [
            (i, i ^ flip) for i in range(lax.axis_size(axis)) if only is None or i in only
        ]
        return lax.ppermute(value, axis, pairs)

    def spread(value, kind):
        pairs = [
            (g * n_cols + c, (g ^ flip_of(kind, c)) * n_cols + c)
            for g in range(layers)
            for c in range(n_cols)
        ]
        return lax.ppermute(value, ("layer", "col"), pairs)

    masks = pltpu.SMEM(pattern.shape, pattern.dtype)
    full_shape = jax.ShapeDtypeStruct((height, width), dtype)
    unit_shape = jax.ShapeDtypeStruct((rows, density.shape[1]), dtype)
    near = pl.pallas_call(
        functools.partial(unit_kernel, share),
        out_shape=unit_shape,
        in_specs=[ANY, ANY],
        out_specs=VMEM,
        scratch_shapes=[masks, pltpu.SemaphoreType.DMA((2,))],
        name="unit",
    )(density, pattern)
    filter_call = pl.pallas_call(
        functools.partial(filter_kernel, share, ALONG_X ^ ALONG_Y),
        out_shape=[
            jax.ShapeDtypeStruct(density.shape, dtype),
            unit_shape,
            full_shape,
            jax.ShapeDtypeStruct((n_rows,) + pattern.shape, pattern.dtype),
        ],
        in_specs=[ANY] * (1 + n_rows),
        out_specs=[VMEM] * 4,
        scratch_shapes=[masks, pltpu.SemaphoreType.DMA((4 + n_rows,))],
        compiler_params=pltpu.CompilerParams(vmem_limit_bytes=16 * 2**20),
        name="filter",
    )
    patterns = [pattern] + [send(pattern, "row", d) for d in range(1, n_rows)]
    filtered, far, full, patterns = filter_call(density, *patterns)
    other_patterns = send(patterns, "col", 1)
    other = send(filtered, "col", 1)

    z1 = send(near, "row", 1)
    b = send(near, "row", outer, middle)
    d = send(z1, "row", outer, middle)
    c = send(b, "row", 1, middle)
    e = send(d, "row", 1, middle)
    z2 = jnp.where(inner, d, c)
    z3 = jnp.where(inner, b, e)

    diagonal = ALONG_X ^ ALONG_Y
    absent = ((3, diagonal),)
    placed = [((0, None), 1, other)]
    late = []
    for k, z in ((1, z1), (2, z2), (3, z3)):
        a_ = spread(z, "a")
        b_ = spread(z, "b")
        w_ = send(far, "row", 1) if k == 1 else spread(a_, "b")
        for kind, value in ((0, z), ("a", a_), ("b", b_), (diagonal, w_)):
            partner = send(value, "col", 1)
            for half, part in enumerate((value, partner)):
                if (k, kind) in absent:
                    late.append(((k, kind), half, part))
                else:
                    placed.append(((k, kind), half, part))
    left_shape = jax.ShapeDtypeStruct((tall, width), dtype)
    partial_shape = jax.ShapeDtypeStruct((tall, width), jnp.float32)

    def add_squares(units, pairs, zeros, full, *held):
        count = len(units)
        layout = tuple(u[:2] for u in units)
        return pl.pallas_call(
            functools.partial(square_kernel, layout, pairs, zeros, share, row_blocks, col_blocks),
            out_shape=[full_shape] + ([] if held else [left_shape]) + [partial_shape],
            in_specs=[HBM] * count + [VMEM] * (1 + len(held)),
            out_specs=[VMEM] * (2 if held else 3),
            input_output_aliases={count: 0, count + 1: 1} if held else {count: 0},
            scratch_shapes=[pltpu.SemaphoreType.DMA((count + 1,))] * 2,
            compiler_params=pltpu.CompilerParams(vmem_limit_bytes=24 * 2**20),
        )(*[u[2] for u in units], full, *held)

    behind = ((1, diagonal), (2, diagonal), (3, "a"), (3, "b"))
    early = [u for u in placed if u[0] not in behind]
    later = [u for u in placed if u[0] in behind]
    full, left, partial = add_squares(early, ((0, 0), (0, ALONG_Y), (1, 0), (2, 0)), (), full)
    full, partial = add_squares(
        later, ((1, ALONG_Y), (2, ALONG_Y), (3, 0), (3, ALONG_Y)), absent, full, partial, left
    )
    tables = [holder.reshape(-1), slot_index, atom_index, patterns, other_patterns]
    n_late = len(late)
    components = derivative.shape[1]
    return pl.pallas_call(
        functools.partial(
            force_kernel, tuple(u[:2] for u in late), absent, n_cols, share, row_blocks, col_blocks
        ),
        out_shape=[jax.ShapeDtypeStruct((components, ATOM_DEV), jnp.float32), full_shape],
        in_specs=[ANY] * len(tables) + [HBM] * n_late + [VMEM] * 4,
        out_specs=[VMEM] * 2,
        input_output_aliases={len(tables) + n_late: 1},
        scratch_shapes=[
            pltpu.VMEM((tall, width), dtype),
            pltpu.VMEM((tall, width), dtype),
            pltpu.VMEM((len(absent) * rows, width), dtype),
            pltpu.VMEM((tall, len(absent) * rows), dtype),
            pltpu.VMEM((components, ATOM_DEV, 8, BS), jnp.float32),
            pltpu.SMEM(slot_index.shape, jnp.int32),
            pltpu.SMEM(slot_index.shape, jnp.int32),
            pltpu.SMEM(slot_index.shape, jnp.int32),
            pltpu.SMEM((2, n_rows) + pattern.shape, jnp.int32),
            pltpu.SemaphoreType.DMA((n_late,)),
            pltpu.SemaphoreType.DMA((len(tables),)),
        ],
        compiler_params=pltpu.CompilerParams(vmem_limit_bytes=24 * 2**20),
        name="force",
    )(*tables, *[u[2] for u in late], full, left, partial, derivative)[0]


def resident_fits(mesh):
    return tuple(mesh.shape[axis] for axis in ("layer", "row", "col")) == RESIDENT_GRID


def solution(mesh):
    specs = dict(
        mesh=mesh,
        in_specs=(
            P("row", "col"),
            P("row", "col"),
            P(("layer", "row", "col"), None),
            P(("layer", "row", "col")),
            P(("layer", "row", "col")),
            P(("layer", "row", "col"), None, None, None),
        ),
        out_specs=P(None, ("layer", "row", "col")),
        check_vma=False,
    )
    if not resident_fits(mesh):
        return jax.shard_map(split_shards, **specs)
    sizes = tuple(mesh.shape[axis] for axis in ("layer", "row", "col"))

    def shards(*args):
        return resident_step(sizes, *args)

    return jax.shard_map(shards, **specs)
```
